32 devices in a mesh: seq: 8 (over y, x, core), wt: 4 (over z).
Axes of the slice: x: 2, y: 2, z: 4, core: 2. Of those that a mesh axis runs over, the one named last changes fastest.
Arguments:
- tokens: bfloat16 [4, 1024, 2048], P('wt', 'seq'), may hold values from -6 to 6
- segment_ids: int32 [4, 1024], P('wt', 'seq'), may hold values from 0 to 15, never falling along the last dimension, each value on 1 to 512 neighbouring positions
- norm_gain: bfloat16 [2048], P('wt'), may hold values from 0.5 to 1.5
- in_weight: bfloat16 [8192, 2048], P('wt'), may hold values from -0.125 to 0.125
- conv_weight: bfloat16 [4, 4096], P(None, 'wt'), may hold values from -3 to 3
- conv_bias: bfloat16 [4096], P('wt'), may hold values from -3 to 3
- proj_weight: bfloat16 [4096, 160], P('wt'), may hold values from -0.09375 to 0.09375
- dt_weight: bfloat16 [4096, 128], P('wt'), may hold values from -0.5 to 0.5
- dt_bias: bfloat16 [4096], P('wt'), may hold values from -9 to 0
- skip_weight: bfloat16 [4096], P('wt'), may hold values from 0.5 to 1.5
- out_weight: bfloat16 [4096, 2048], P('wt'), may hold values from -0.1875 to 0.1875
- cotangent: bfloat16 [4, 1024, 2048], P('wt', 'seq'), may hold values from -6 to 6
Outputs:
- block_output: bfloat16 [4, 1024, 2048], P('wt', 'seq')
- token_grad: bfloat16 [4, 1024, 2048], P('wt', 'seq')
- gain_grad: float32 [2048], P('wt')
- in_grad: float32 [8192, 2048], P('wt')
- conv_weight_grad: float32 [4, 4096], P(None, 'wt')
- conv_bias_grad: float32 [4096], P('wt')
- proj_grad: float32 [4096, 160], P('wt')
- dt_grad: float32 [4096, 128], P('wt')
- dt_bias_grad: float32 [4096], P('wt')
- skip_grad: float32 [4096], P('wt')
- out_grad: float32 [4096, 2048], P('wt')
The draws below stay inside these ranges and needn't reach their ends.
Inputs may be any that keep to these rules, and one draw needn't show every extreme that they name: `segment_ids`: within each sequence the ids never fall; every number of 0 to 15 marks one document of 1 to 512 tokens, and one document has exactly 512.
All inputs are finite; a program needn't handle non-finite values.
Results may differ from the reference program's by a relative error of at most 0.011.
Values may be sent and summed in bfloat16 or wider, within the bound.
No kernel may reach another device: no remote copies, remote signals or barrier semaphores. Data moves between devices by JAX's collectives and lax.ppermute only.
A program may use at most 248 MiB of HBM per device.

```python
import math
import jax
import jax.numpy as jnp
import numpy as np
from jax import lax

D = 2048
INNER = 4096
STATE = 16
RANK = 128
KERNEL = 4
DOCS = 16
LENGTH = 1024
MOST = 512
SEQS = 4


def block_levels(own_key, dims, cuts, least, high):
    gain, own = 1.0, jax.random.fold_in(own_key, 6)
    for position, blocks in cuts:
        draws = jnp.exp(jax.random.uniform(jax.random.fold_in(own, position), (blocks,), jnp.float32, least / len(cuts), high / len(cuts)))
        gain = gain * jnp.repeat(draws, dims[position] // blocks).reshape([-1 if axis == position else 1 for axis in range(len(dims))])
    return gain


def length_profile(amount, total, most, skew):
    portions = [(1 << 20) // math.isqrt(standing ** skew) + 1 for standing in range(2, amount + 1)]
    surplus, holding = total - most - (amount - 1), [1] * (amount - 1)
    while surplus > 0:
        candidates = [i for i in range(amount - 1) if holding[i] < most]
        pool, remaining = sum([portions[i] for i in candidates]), surplus
        for i in candidates:
            addition = min(most - holding[i], max(1, remaining * portions[i] // pool), surplus)
            holding[i] = holding[i] + addition
            surplus = surplus - addition
    return np.array([most] + holding)


def ragged(rng, number_of, total, limit, skew):
    if number_of == 2:
        one = jax.random.randint(rng, (), max(1, total - limit), min(limit, total - 1) + 1)
        return jnp.stack([one, total - one])
    tallies = jnp.asarray(length_profile(number_of, total, limit, skew), jnp.int32)
    pairs = (number_of - 1) // 2
    source_of, sink = tallies[1:1 + 2 * pairs:2], tallies[2:2 + 2 * pairs:2]
    slack = jnp.minimum(source_of - 1, limit - sink)
    shifted = jax.random.randint(jax.random.fold_in(rng, 1), (pairs,), 0, 1 << 20) % (slack + 1)
    tallies = tallies.at[1:1 + 2 * pairs:2].set(source_of - shifted).at[2:2 + 2 * pairs:2].set(sink + shifted)
    return tallies[jax.random.permutation(jax.random.fold_in(rng, 2), number_of)]


def noise(own_key, extent, scale, bound, split=(), dtype=jnp.bfloat16):
    result = jax.random.normal(own_key, extent, jnp.float32) * scale
    if len(split) > 0:
        result = block_levels(own_key, extent, split, -0.22, 0.18) * result
    return jnp.clip(result, min=-bound, max=bound).astype(dtype)


def setup_inputs(seed: int = 0) -> dict:
    arg_keys = jax.random.split(jax.random.key(seed), 13)
    tokens = noise(arg_keys[0], (SEQS, LENGTH, D), 1.0, 6.0, ((0, 4), (1, 8)))
    segment_ids = jax.vmap(lambda own: jnp.searchsorted(jnp.cumsum(ragged(own, DOCS, LENGTH, MOST, 2)), jnp.arange(LENGTH), side="right"))(jax.random.split(arg_keys[1], SEQS)).reshape((SEQS, LENGTH)).astype(jnp.int32)
    norm_gain = jnp.clip(1.0 + 0.1 * jax.random.normal(arg_keys[2], (D,), jnp.float32), 0.5, 1.5).astype(jnp.bfloat16)
    in_weight = noise(arg_keys[3], (2 * INNER, D), D ** -0.5, 0.125, ((0, 4),))
    conv_weight = noise(arg_keys[4], (KERNEL, INNER), KERNEL ** -0.5, 3.0, ((1, 4),))
    conv_bias = noise(arg_keys[5], (INNER,), 0.5, 3.0, ((0, 4),))
    proj_weight = noise(arg_keys[6], (INNER, 2 * STATE + RANK), INNER ** -0.5, 0.09375, ((0, 4),))
    dt_weight = noise(arg_keys[7], (INNER, RANK), RANK ** -0.5, 0.5, ((0, 4),))
    dt_bias = jnp.clip(-9.0 + 9.0 * jax.random.uniform(arg_keys[8], (INNER,), jnp.float32) ** block_levels(arg_keys[8], (INNER,), ((0, 4),), -0.2, 0.2), -9.0, 0.0).astype(jnp.bfloat16)
    skip_weight = jnp.clip(1.0 + 0.1 * jax.random.normal(arg_keys[9], (INNER,), jnp.float32), 0.5, 1.5).astype(jnp.bfloat16)
    out_weight = noise(arg_keys[10], (INNER, D), (INNER // 4) ** -0.5, 0.1875, ((0, 4),))
    cotangent = noise(arg_keys[11], (SEQS, LENGTH, D), 1.0, 6.0, ((0, 4), (1, 8)))
    return dict(tokens=tokens, segment_ids=segment_ids, norm_gain=norm_gain, in_weight=in_weight, conv_weight=conv_weight, conv_bias=conv_bias, proj_weight=proj_weight, dt_weight=dt_weight, dt_bias=dt_bias, skip_weight=skip_weight, out_weight=out_weight, cotangent=cotangent)


norm_eps = 1e-05

@jax.custom_vjp
def low(v):
    return lax.optimization_barrier(v.astype(jnp.bfloat16)).astype(jnp.float32)

@jax.custom_vjp
def low_back(v):
    return v

def low_keep(v):
    return (low(v), None)

def low_pass(kept, grad):
    return (grad,)

def back_keep(v):
    return (v, None)

def back_low(kept, grad):
    return (low(grad),)
low.defvjp(low_keep, low_pass)
low_back.defvjp(back_keep, back_low)

def matmul(left, right):
    return jnp.dot(left, right, precision=lax.Precision.HIGHEST, preferred_element_type=jnp.float32)

def state_step(state_now, inputs):
    keep_now, rate_now, value_now, key_now, query_now = inputs
    decay = 1.0 - key_now[:, None] * key_now[:, None] * rate_now[None, :]
    state_now = keep_now * decay * state_now + key_now[:, None] * (rate_now * value_now)[None, :]
    return (state_now, lax.optimization_barrier(jnp.sum(query_now[:, None] * state_now, axis=0)))

def run_piece(state_now, piece):
    return lax.scan(state_step, state_now, piece)

def recurrence(state_now, keep_mask, rate_vec, conv_out, key_vec, query_vec):
    length = keep_mask.shape[0]
    block_len = math.gcd(64, length)
    blocked = tuple((member.reshape((length // block_len, block_len) + member.shape[1:]) for member in (keep_mask, rate_vec, conv_out, key_vec, query_vec)))
    state_now, outputs = lax.scan(jax.checkpoint(run_piece), state_now, blocked)
    return (state_now, outputs.reshape(length, outputs.shape[-1]))

def sequence(features, segments, norm_gain, in_weight, conv_weight, conv_bias, proj_weight, dt_weight, dt_bias, skip_weight, out_weight):
    length = features.shape[0]
    inv_rms = lax.rsqrt(lax.optimization_barrier(jnp.mean(features * features, axis=1, keepdims=True)) + norm_eps)
    normed = low(features * inv_rms * norm_gain)
    projected_in = low_back(matmul(normed, in_weight.T))
    value_rows = low(projected_in[:, :INNER])
    gate_pre = projected_in[:, INNER:]
    padded = jnp.pad(value_rows, ((KERNEL - 1, 0), (0, 0)))
    padded_ids = jnp.pad(segments, (KERNEL - 1, 0))
    conv_sum = conv_bias
    for offset in range(KERNEL):
        same_doc = (padded_ids[offset:offset + length] == segments).astype(jnp.float32)
        conv_sum = conv_sum + conv_weight[offset] * padded[offset:offset + length] * same_doc[:, None]
    conv_out = low(jax.nn.silu(conv_sum))
    projected = low_back(matmul(conv_out, proj_weight))
    query_vec = projected[:, :STATE]
    key_vec = projected[:, STATE:2 * STATE]
    low_rank = low(projected[:, 2 * STATE:])
    beta_pre = low_back(matmul(low_rank, dt_weight.T))
    beta_rate = jax.nn.softplus(beta_pre + dt_bias)
    rate_vec = beta_rate / (1.0 + beta_rate * lax.optimization_barrier(jnp.sum(key_vec * key_vec, axis=1, keepdims=True)))
    keep_mask = (padded_ids[KERNEL - 2:KERNEL - 2 + length] == segments).astype(jnp.float32)
    start_state = jnp.zeros((STATE, INNER), jnp.float32)
    _, core_out = recurrence(start_state, keep_mask, rate_vec, conv_out, key_vec, query_vec)
    gated = low((core_out + skip_weight * conv_out) * jax.nn.silu(gate_pre))
    return features + matmul(gated, out_weight)

def reference(tokens, segment_ids, norm_gain, in_weight, conv_weight, conv_bias, proj_weight, dt_weight, dt_bias, skip_weight, out_weight, cotangent):
    weights_full = tuple((member.astype(jnp.float32) for member in (norm_gain, in_weight, conv_weight, conv_bias, proj_weight, dt_weight, dt_bias, skip_weight, out_weight)))

    def forward(features, *weights):

        def run_sequence(sample):
            return jax.checkpoint(sequence)(sample[0], sample[1], *weights)
        return lax.map(run_sequence, (features, segment_ids))
    output, pullback = jax.vjp(forward, tokens.astype(jnp.float32), *weights_full)
    gradients = pullback(cotangent.astype(jnp.float32))
    return (output.astype(jnp.bfloat16), gradients[0].astype(jnp.bfloat16), gradients[1], gradients[2], gradients[3], gradients[4], gradients[5], gradients[6], gradients[7], gradients[8], gradients[9])
```

```python
import jax
import jax.numpy as jnp
from jax import lax
from jax.experimental import pallas as pl
from jax.experimental.pallas import tpu as pltpu
from jax.sharding import PartitionSpec as P

STATE = 16
KERNEL = 4
HALO = KERNEL - 1
GROUP = 8
LANES = 128
PACKET = 16
EPS = 1e-05
F32 = jnp.float32
BF16 = jnp.bfloat16


def circular(value, axis, steps):
    count = lax.axis_size(axis)
    return lax.ppermute(value, axis, [(i, (i + steps) % count) for i in range(count)])


def small_gather(value, axis):
    return [value] + [circular(value, axis, k) for k in range(1, lax.axis_size(axis))]


def in_order(parts, axis):
    count, mine = lax.axis_size(axis), lax.axis_index(axis)
    out = jnp.zeros((count,) + parts[0].shape, parts[0].dtype)
    for k, part in enumerate(parts):
        out = lax.dynamic_update_index_in_dim(out, part, (mine - k) % count, 0)
    return out


def line_gather(value, axis):
    count, mine = lax.axis_size(axis), lax.axis_index(axis)
    up, down = [value], [value]
    for m in range(1, count):
        up.append(lax.ppermute(up[-1], axis, [(i, i + 1) for i in range(m - 1, count - 1)]))
        down.append(lax.ppermute(down[-1], axis, [(i, i - 1) for i in range(1, count - m + 1)]))
    return [value] + [jnp.where(mine >= k, up[k], down[count - k]) for k in range(1, count)]


def line_scatter(terms, axis):
    count, mine = lax.axis_size(axis), lax.axis_index(axis)
    parts = [lax.dynamic_index_in_dim(terms, (mine - k) % count, 0, keepdims=False) for k in range(count)]
    up = down = None
    for m in range(1, count):
        to_up = parts[m] if up is None else parts[m] + up.astype(F32)
        to_down = parts[count - m] if down is None else parts[count - m] + down.astype(F32)
        up = lax.ppermute(to_up.astype(BF16), axis, [(i, i + 1) for i in range(m)])
        down = lax.ppermute(to_down.astype(BF16), axis, [(i, i - 1) for i in range(count - m, count)])
    return parts[0] + up.astype(F32) + down.astype(F32)


def all_sum(value, axis):
    count = lax.axis_size(axis)
    bit = 1
    while bit < count:
        value = value + lax.ppermute(value, axis, [(i, i ^ bit) for i in range(count)])
        bit *= 2
    return value


def shifted(value, axis, steps):
    count = lax.axis_size(axis)
    leading, last = (max(0, -steps), min(count, count - steps))
    return lax.ppermute(value, axis, [(source, source + steps) for source in range(leading, last)])


def to_users(slots, axis):
    count, mine = lax.axis_size(axis), lax.axis_index(axis)
    half = count // 2
    first = lax.ppermute(
        jnp.where(mine < half, slots[0], slots[1]),
        axis,
        [(j, 2 * j if j < half else (2 * j + 1) % count) for j in range(count)],
    )
    second = lax.ppermute(
        jnp.where(mine < half, slots[1], slots[0]),
        axis,
        [(j, 2 * j + 1 if j < half else (2 * j) % count) for j in range(count)],
    )
    even = mine % 2 == 0
    return jnp.where(even, first, second), jnp.where(even, second, first)


def to_owners(block, axis, offset):
    count = lax.axis_size(axis)
    return [
        lax.ppermute(block, axis, [(w, offset + w // 2) for w in range(slot, count, 2)])
        for slot in range(2)
    ]


def tiles_of(width):
    return [pl.ds(at * LANES, LANES) for at in range(width // LANES)]


def row_sums(parts):
    row = lax.broadcasted_iota(jnp.int32, (GROUP, LANES), 0)
    low4, low2, low1 = row < 4, (row & 2) == 0, (row & 1) == 0
    fours = [
        jnp.where(low4, parts[j], parts[j + 4])
        + pltpu.roll(jnp.where(low4, parts[j + 4], parts[j]), 4, 0)
        for j in range(4)
    ]
    twos = [
        jnp.where(low2, fours[j] + pltpu.roll(fours[j], 6, 0), fours[j + 2] + pltpu.roll(fours[j + 2], 2, 0))
        for j in range(2)
    ]
    return jnp.where(low1, twos[0] + pltpu.roll(twos[0], 7, 0), twos[1] + pltpu.roll(twos[1], 1, 0))


def lane_sums(lanes_ref):
    ones = jnp.ones((GROUP, LANES), F32)
    return lax.dot_general(
        ones, lanes_ref[...], (((1,), (1,)), ((), ())), precision=lax.Precision.HIGHEST, preferred_element_type=F32
    )


def summary_kernel(key_ref, query_ref, keep_ref, rate_ref, feed_ref, grad_ref, decay_ref, state_ref, adjoint_ref):
    steps, width = rate_ref.shape
    tiles = tiles_of(width)
    keep0, key0 = keep_ref[...], key_ref[...]

    def body(i, carry):
        key, square, query, keep, decay, state, adjoint = carry
        decay, state, adjoint = list(decay), list(state), list(adjoint)
        rows = pl.ds(pl.multiple_of(i * GROUP, GROUP), GROUP)
        rate = [rate_ref[rows, tile] for tile in tiles]
        feed = [feed_ref[rows, tile] for tile in tiles]
        grad = [grad_ref[rows, tile] for tile in tiles]
        for j in range(GROUP):
            key_now, square_now = key[:, j : j + 1], square[:, j : j + 1]
            query_now, keep_now = query[:, j : j + 1], keep[:, j : j + 1]
            for at in range(len(tiles)):
                factor = keep_now - square_now * rate[at][j : j + 1]
                state[at] = factor * state[at] + key_now * feed[at][j : j + 1]
                decay[at] = factor * decay[at]
                adjoint[at] = adjoint[at] + decay[at] * (query_now * grad[at][j : j + 1])
        key, square, query, keep = (pltpu.roll(part, steps - GROUP, 1) for part in (key, square, query, keep))
        return key, square, query, keep, tuple(decay), tuple(state), tuple(adjoint)

    zero = jnp.zeros((STATE, LANES), F32)
    count = len(tiles)
    start = (key0, keep0 * key0 * key0, query_ref[...], keep0, (zero + 1.0,) * count, (zero,) * count, (zero,) * count)
    _, _, _, _, decay, state, adjoint = lax.fori_loop(0, steps // GROUP, body, start)
    for at, tile in enumerate(tiles):
        decay_ref[0, :, tile] = decay[at].astype(decay_ref.dtype)
        state_ref[0, :, tile] = state[at].astype(state_ref.dtype)
        adjoint_ref[0, :, tile] = adjoint[at].astype(adjoint_ref.dtype)


def forward_kernel(key_ref, query_ref, keep_ref, rate_ref, feed_ref, grad_ref, start_ref, out_ref, before_ref, dquery_ref, lanes_ref):
    steps, width = rate_ref.shape
    tiles = tiles_of(width)
    keep0, key0 = keep_ref[...], key_ref[...]

    def body(i, carry):
        key, square, query, keep, state = carry
        state = list(state)
        base = pl.multiple_of(i * GROUP, GROUP)
        rows = pl.ds(base, GROUP)
        rate = [rate_ref[rows, tile] for tile in tiles]
        feed = [feed_ref[rows, tile] for tile in tiles]
        grad = [grad_ref[rows, tile] for tile in tiles]
        weighed = [[] for _ in tiles]
        for j in range(GROUP):
            key_now, square_now = key[:, j : j + 1], square[:, j : j + 1]
            query_now, keep_now = query[:, j : j + 1], keep[:, j : j + 1]
            total = None
            for at, tile in enumerate(tiles):
                before_ref[0, 0, base + j, :, tile] = state[at]
                factor = keep_now - square_now * rate[at][j : j + 1]
                state[at] = factor * state[at] + key_now * feed[at][j : j + 1]
                out = query_now * state[at]
                weighed[at].append(out[:GROUP] + out[GROUP:])
                term = grad[at][j : j + 1] * state[at]
                total = term if total is None else total + term
            lanes_ref[pl.ds(pl.multiple_of((base + j) * STATE, STATE), STATE), :] = total
        for at, tile in enumerate(tiles):
            out_ref[rows, tile] = row_sums(weighed[at])
        key, square, query, keep = (pltpu.roll(part, steps - GROUP, 1) for part in (key, square, query, keep))
        return key, square, query, keep, tuple(state)

    start = tuple(start_ref[0, :, tile] for tile in tiles)
    carry = (key0, keep0 * key0 * key0, query_ref[...], keep0, start)
    lax.fori_loop(0, steps // GROUP, body, carry)
    dquery_ref[...] = lane_sums(lanes_ref)


def backward_kernel(key_ref, query_ref, keep_ref, rate_ref, feed_ref, grad_ref, before_ref, start_ref, along_ref, across_ref, dkey_ref, lanes_ref):
    steps, width = rate_ref.shape
    tiles = tiles_of(width)
    groups = steps // GROUP
    keep0, key0 = keep_ref[...], key_ref[...]

    def body(i, carry):
        key, square, twice, query, keep, adjoint = carry
        key, square, twice, query, keep = (pltpu.roll(part, GROUP, 1) for part in (key, square, twice, query, keep))
        adjoint = list(adjoint)
        base = pl.multiple_of((groups - 1 - i) * GROUP, GROUP)
        rows = pl.ds(base, GROUP)
        rate = [rate_ref[rows, tile] for tile in tiles]
        feed = [feed_ref[rows, tile] for tile in tiles]
        grad = [grad_ref[rows, tile] for tile in tiles]
        along, across = [[None] * GROUP for _ in tiles], [[None] * GROUP for _ in tiles]
        for j in reversed(range(GROUP)):
            key_now, square_now, twice_now = key[:, j : j + 1], square[:, j : j + 1], twice[:, j : j + 1]
            query_now, keep_now = query[:, j : j + 1], keep[:, j : j + 1]
            plain = crossed = None
            for at, tile in enumerate(tiles):
                rate_now = rate[at][j : j + 1]
                full = adjoint[at] + query_now * grad[at][j : j + 1]
                product = full * before_ref[0, 0, base + j, :, tile]
                one, two = key_now * full, square_now * product
                along[at][j] = one[:GROUP] + one[GROUP:]
                across[at][j] = two[:GROUP] + two[GROUP:]
                three, four = full * feed[at][j : j + 1], product * rate_now
                plain = three if plain is None else plain + three
                crossed = four if crossed is None else crossed + four
                adjoint[at] = (keep_now - square_now * rate_now) * full
            lanes_ref[pl.ds(pl.multiple_of((base + j) * STATE, STATE), STATE), :] = plain - twice_now * crossed
        for at, tile in enumerate(tiles):
            along_ref[rows, tile] = row_sums(along[at])
            across_ref[rows, tile] = row_sums(across[at])
        return key, square, twice, query, keep, tuple(adjoint)

    start = tuple(start_ref[0, :, tile] for tile in tiles)
    carry = (
        key0,
        keep0 * key0 * key0,
        2.0 * keep0 * key0,
        query_ref[...],
        keep0,
        start,
    )
    lax.fori_loop(0, groups, body, carry)
    dkey_ref[...] = lane_sums(lanes_ref)


class Mixer:
    def __init__(self, seqs, steps, width):
        self.seqs, self.steps, self.width = seqs, steps, width
        self.part = width
        self.grid = (seqs, width // self.part)
        self.column = pl.BlockSpec((STATE, steps), lambda i, e: (0, i))
        self.row = pl.BlockSpec((steps, self.part), lambda i, e: (i, e))
        self.state = pl.BlockSpec((1, STATE, self.part), lambda i, e: (i, 0, e))
        self.states = pl.BlockSpec((1, 1, steps, STATE, self.part), lambda i, e: (i, e, 0, 0, 0))
        self.sums = pl.BlockSpec((GROUP, steps * STATE), lambda i, e: (e, i))
        self.all_sums = jax.ShapeDtypeStruct((self.grid[1] * GROUP, seqs * steps * STATE), F32)
        self.lanes = pltpu.VMEM((steps * STATE, LANES), F32)
        self.rows = jax.ShapeDtypeStruct((seqs * steps, width), F32)

    def call(self, kernel, name, in_specs, out_specs, out_shape, ops, nbytes, scratch=()):
        elements = self.seqs * self.steps * STATE * self.width
        return pl.pallas_call(
            kernel,
            grid=self.grid,
            in_specs=in_specs,
            out_specs=out_specs,
            out_shape=out_shape,
            name=name,
            scratch_shapes=scratch,
            cost_estimate=pl.CostEstimate(flops=ops * elements, bytes_accessed=nbytes, transcendentals=0),
            compiler_params=pltpu.CompilerParams(
                dimension_semantics=("arbitrary", "arbitrary"), vmem_limit_bytes=48 * 1024 * 1024
            ),
        )

    def summary(self, *args):
        shape = jax.ShapeDtypeStruct((self.seqs, STATE, self.width), F32)
        specs = [self.column] * 3 + [self.row] * 3
        nbytes = 12 * self.seqs * self.steps * self.width
        return self.call(summary_kernel, "block_summary", specs, [self.state] * 3, [shape] * 3, 11, nbytes)(*args)

    def forward(self, *args):
        states = jax.ShapeDtypeStruct((self.seqs, self.grid[1], self.steps, STATE, self.part), F32)
        specs = [self.column] * 3 + [self.row] * 3 + [self.state]
        nbytes = (16 + 4 * STATE) * self.seqs * self.steps * self.width
        return self.call(
            forward_kernel,
            "states",
            specs,
            [self.row, self.states, self.sums],
            [self.rows, states, self.all_sums],
            10,
            nbytes,
            [self.lanes],
        )(*args)

    def columns(self, sums):
        return sum(sums[at * GROUP] for at in range(self.grid[1])).reshape(-1, STATE).T

    def backward(self, *args):
        specs = [self.column] * 3 + [self.row] * 3 + [self.states, self.state]
        nbytes = (20 + 4 * STATE) * self.seqs * self.steps * self.width
        return self.call(
            backward_kernel,
            "adjoints",
            specs,
            [self.row, self.row, self.sums],
            [self.rows, self.rows, self.all_sums],
            20,
            nbytes,
            [self.lanes],
        )(*args)


def dot(left, right, over_left, over_right):
    return lax.dot_general(left, right, (((over_left,), (over_right,)), ((), ())), preferred_element_type=F32)


def inverse_rms(features):
    return lax.rsqrt(jnp.mean(features * features, axis=1, keepdims=True) + EPS)


def on_device(
    tokens,
    segment_ids,
    norm_gain,
    in_weight,
    conv_weight,
    conv_bias,
    proj_weight,
    dt_weight,
    dt_bias,
    skip_weight,
    out_weight,
    cotangent,
):
    groups, blocks = lax.axis_size("wt"), lax.axis_size("seq")
    mine, block = lax.axis_index("wt"), lax.axis_index("seq")
    own, own_cot, own_ids = tokens[0], cotangent[0], segment_ids[0] + 1
    length, model = own.shape
    width = out_weight.shape[0]
    rows = groups * length
    taps, bias32 = conv_weight.astype(F32), conv_bias.astype(F32)
    dt_bias32, skip32 = dt_bias.astype(F32), skip_weight.astype(F32)

    edge_ids = jnp.pad(own_ids[length - HALO :].astype(BF16), (0, model - HALO))
    packet = jnp.concatenate([own[length - HALO :], edge_ids[None]], axis=0)
    packet = shifted(packet, "seq", 1)
    all_ids = jnp.concatenate([packet[HALO, :HALO], own_ids.astype(BF16)])
    packet = jnp.concatenate(
        [
            packet[:HALO],
            jnp.pad(all_ids, (0, model - HALO - length))[None],
            jnp.pad(norm_gain, (0, model - norm_gain.shape[0]))[None],
            jnp.zeros((PACKET - HALO - 2, model), BF16),
        ],
        axis=0,
    )
    packets = in_order(small_gather(packet, "wt"), "wt")

    chunk = width // blocks
    slots = [
        lax.dynamic_slice_in_dim(in_weight, slot * width + block * chunk, chunk, 0) for slot in range(2)
    ]
    value_chunk, gate_chunk = to_users(slots, "wt")
    value_weight = lax.all_gather(value_chunk, "seq", axis=0, tiled=True)
    gate_weight = lax.all_gather(gate_chunk, "seq", axis=0, tiled=True)

    gathered = in_order(line_gather(own, "wt"), "wt").reshape(rows, model)
    cots = in_order(line_gather(own_cot, "wt"), "wt").reshape(rows, model)

    gain32 = packets[:, HALO + 1, : model // groups].astype(F32).reshape(model)

    features = jnp.concatenate([gathered, packets.reshape(groups * PACKET, model)], axis=0).astype(F32)
    normed_all = (features * inverse_rms(features) * gain32).astype(BF16)
    normed = normed_all[:rows]
    values_all = dot(normed_all, value_weight, 1, 1).astype(BF16)
    gate_pre = dot(normed, gate_weight, 1, 1)
    extended = jnp.concatenate(
        [
            values_all[rows:].reshape(groups, PACKET, width)[:, :HALO],
            values_all[:rows].reshape(groups, length, width),
        ],
        axis=1,
    ).astype(F32)
    ids = packets[:, HALO, : HALO + length]
    same_doc = [(ids[:, k : k + length] == ids[:, HALO:]).astype(F32)[:, :, None] for k in range(KERNEL)]
    conv_sum = bias32 + sum(taps[k] * extended[:, k : k + length] * same_doc[k] for k in range(KERNEL))
    conv_out = jax.nn.silu(conv_sum).astype(BF16).reshape(rows, width)
    conv_vals = conv_out.astype(F32)

    projected = all_sum(dot(proj_weight, conv_out, 0, 1), "wt")
    query, key = projected[:STATE], projected[STATE : 2 * STATE]
    low_rank = projected[2 * STATE :].astype(BF16)
    keep = same_doc[KERNEL - 2].reshape(1, rows)
    keeps = jnp.broadcast_to(keep, (STATE, rows))
    key_square = jnp.sum(key * key, axis=0)[:, None]
    beta_in = dot(low_rank, dt_weight, 0, 1) + dt_bias32
    beta = jax.nn.softplus(beta_in)
    shrink = 1.0 / (1.0 + beta * key_square)
    rate = beta * shrink
    feed = rate * conv_vals
    d_gated = dot(cots, out_weight, 1, 1)
    sigma = jax.nn.sigmoid(gate_pre)
    gate = gate_pre * sigma
    d_mixed = d_gated * gate

    mixer = Mixer(groups, length, width)
    summary = jnp.stack([part.astype(BF16) for part in mixer.summary(key, query, keeps, rate, feed, d_mixed)])
    everything = lax.all_gather(summary, "seq").astype(F32)
    state_in = jnp.zeros((groups, STATE, width), F32)
    grad_in = jnp.zeros((groups, STATE, width), F32)
    for at in range(blocks):
        state_in = jnp.where(at < block, everything[at, 0] * state_in + everything[at, 1], state_in)
        back = blocks - 1 - at
        grad_in = jnp.where(back > block, everything[back, 0] * grad_in + everything[back, 2], grad_in)

    core_out, before, d_query = mixer.forward(key, query, keeps, rate, feed, d_mixed, state_in)
    d_query = mixer.columns(d_query)
    mixed = core_out + skip32 * conv_vals
    gated = (mixed * gate).astype(BF16)
    d_gate = (d_gated * mixed * (sigma * (1.0 + gate_pre * (1.0 - sigma)))).astype(BF16)
    skip_part = jnp.sum(d_mixed * conv_vals, axis=0)
    out_parts = dot(gated, out_weight, 1, 0).reshape(groups, length, model)
    block_output = (own.astype(F32) + line_scatter(out_parts, "wt")).astype(BF16)
    out_share = dot(gated, cots, 0, 0)
    out_chunk = lax.psum_scatter(out_share.astype(BF16), "seq", scatter_dimension=0, tiled=True)
    gate_share = dot(d_gate, normed, 0, 0)
    gate_part = lax.psum_scatter(gate_share.astype(BF16), "seq", scatter_dimension=0, tiled=True)
    gate_slots = to_owners(gate_part, "wt", groups // 2)

    along, across, d_key = mixer.backward(key, query, keeps, rate, feed, d_mixed, before, grad_in)
    d_key = mixer.columns(d_key)
    d_rate = conv_vals * along - across
    d_beta = d_rate * shrink * shrink
    from_square = jnp.sum(d_beta * beta * beta, axis=1)
    d_key = d_key - 2.0 * key * from_square
    d_bias = d_beta * jax.nn.sigmoid(beta_in)
    dt_bias_part = jnp.sum(d_bias, axis=0)
    d_beta_low = d_bias.astype(BF16)
    d_low_rank = dot(dt_weight, d_beta_low, 0, 1)
    d_projected = all_sum(jnp.concatenate([d_query, d_key, d_low_rank], axis=0), "wt").astype(BF16)
    dt_part = dot(d_beta_low, low_rank, 0, 1)
    proj_part = dot(conv_out, d_projected, 0, 1)
    d_value = d_mixed * skip32 + rate * along + dot(d_projected, proj_weight, 0, 1)

    sigma_conv = jax.nn.sigmoid(conv_sum)
    d_conv = d_value.reshape(groups, length, width) * (sigma_conv * (1.0 + conv_sum * (1.0 - sigma_conv)))
    conv_bias_part = jnp.sum(d_conv, axis=(0, 1))
    masked = [d_conv * same_doc[k] for k in range(KERNEL)]
    conv_part = jnp.stack([jnp.sum(masked[k] * extended[:, k : k + length], axis=(0, 1)) for k in range(KERNEL)])
    d_extended = sum(
        jnp.pad(taps[k] * masked[k], ((0, 0), (k, HALO - k), (0, 0))) for k in range(KERNEL)
    )
    returned = shifted(d_extended[:, :HALO], "seq", -1)
    d_rows = d_extended[:, HALO:] + jnp.pad(returned, ((0, 0), (length - HALO, 0), (0, 0)))
    d_rows = d_rows.astype(BF16).reshape(rows, width)

    value_share = dot(d_rows, normed, 0, 0)
    value_part = lax.psum_scatter(value_share.astype(BF16), "seq", scatter_dimension=0, tiled=True)
    value_slots = to_owners(value_part, "wt", 0)
    in_chunk = jnp.stack([value_slots[slot] + gate_slots[slot] for slot in range(2)])

    d_normed_parts = (dot(d_rows, value_weight, 1, 0) + dot(d_gate, gate_weight, 1, 0)).reshape(groups, length, model)
    d_normed = line_scatter(d_normed_parts, "wt")
    own32 = own.astype(F32)
    inv_rms = inverse_rms(own32)
    weighted = d_normed * gain32
    along_features = jnp.mean(own32 * weighted, axis=1, keepdims=True)
    token_grad = (own_cot.astype(F32) + inv_rms * weighted - own32 * (inv_rms * inv_rms * inv_rms) * along_features).astype(BF16)
    gain_part = jnp.sum(d_normed * own32 * inv_rms, axis=0)
    gain_part = lax.psum_scatter(gain_part, "wt", scatter_dimension=0, tiled=True)

    gain_grad, conv_grad, conv_bias_grad, proj_grad, dt_grad, dt_bias_grad, skip_grad = lax.psum(
        (gain_part, conv_part, conv_bias_part, proj_part, dt_part, dt_bias_part, skip_part), "seq"
    )
    out_grad = lax.all_gather(out_chunk, "seq", axis=0, tiled=True).astype(F32)
    in_grad = lax.all_gather(in_chunk, "seq", axis=1, tiled=True).astype(F32).reshape(2 * width, model)
    return (
        block_output[None],
        token_grad[None],
        gain_grad,
        in_grad,
        conv_grad,
        conv_bias_grad,
        proj_grad,
        dt_grad,
        dt_bias_grad,
        skip_grad,
        out_grad,
    )


def solution(mesh):
    return jax.shard_map(
        on_device,
        mesh=mesh,
        in_specs=(
            P("wt", "seq", None),
            P("wt", "seq"),
            P("wt"),
            P("wt", None),
            P(None, "wt"),
            P("wt"),
            P("wt", None),
            P("wt", None),
            P("wt"),
            P("wt"),
            P("wt", None),
            P("wt", "seq", None),
        ),
        out_specs=(
            P("wt", "seq", None),
            P("wt", "seq", None),
            P("wt"),
            P("wt", None),
            P(None, "wt"),
            P("wt"),
            P("wt", None),
            P("wt", None),
            P("wt"),
            P("wt"),
            P("wt", None),
        ),
        check_vma=False,
    )
```

```python
import functools

import jax
import jax.numpy as jnp
from jax import lax
from jax.experimental import pallas as pl
from jax.experimental.pallas import tpu as pltpu
from jax.sharding import PartitionSpec as P

STATE = 16
KERNEL = 4
HALO = KERNEL - 1
GROUP = 8
LANES = 128
PACKET = 16
EPS = 1e-05
DEPTH = 4
VECTOR_COST = 1
F32 = jnp.float32
BF16 = jnp.bfloat16


def circular(value, axis, steps):
    count = lax.axis_size(axis)
    return lax.ppermute(value, axis, [(i, (i + steps) % count) for i in range(count)])


def small_gather(value, axis):
    return [value] + [circular(value, axis, k) for k in range(1, lax.axis_size(axis))]


def in_order(parts, axis):
    count, mine = lax.axis_size(axis), lax.axis_index(axis)
    out = jnp.zeros((count,) + parts[0].shape, parts[0].dtype)
    for k, part in enumerate(parts):
        out = lax.dynamic_update_index_in_dim(out, part, (mine - k) % count, 0)
    return out


def tie(*values):
    return lax.optimization_barrier(values)


def far_gather(value, axis):
    pieces = {0: value}
    for bit in bits_of(axis)[:-1]:
        pieces.update({r | bit: across_bit(part, axis, bit) for r, part in pieces.items()})
    del pieces[0]
    return pieces


def near_gather(pieces, axis):
    return {r | 1: across_bit(part, axis, 1) for r, part in pieces.items()}


def near_sum(kept, comes):
    return [kept[at] + comes[at].astype(F32) for at in range(kept.shape[0])]


def far_sum(terms, axis, sent=None, hold=lambda part: part):
    terms = {2 * at: part for at, part in enumerate(terms)}
    for bit in reversed(bits_of(axis)[:-1]):
        for r in sorted(terms):
            if r & bit:
                part = terms.pop(r)
                part = part.astype(BF16) if sent is None or len(terms) > 1 else sent
                terms[r ^ bit] = terms[r ^ bit] + hold(across_bit(part, axis, bit)).astype(F32)
    return terms[0]


def all_sum(value, sent, axis):
    for k in range(1, lax.axis_size(axis)):
        value = value + circular(sent, axis, k).astype(F32)
    return value


def direct_scatter(terms, axis):
    count, mine = lax.axis_size(axis), lax.axis_index(axis)
    parts = [lax.dynamic_index_in_dim(terms, (mine + k) % count, 0, keepdims=False) for k in range(count)]
    return parts[0], [circular(parts[k].astype(BF16), axis, k) for k in range(1, count)]


def across_bit(value, axis, bit):
    return lax.ppermute(value, axis, [(i, i ^ bit) for i in range(lax.axis_size(axis))])


def bits_of(axis):
    count = lax.axis_size(axis)
    return [count >> (at + 1) for at in range(count.bit_length() - 1)]


def bit_gather(value, axis):
    first, second, *rest = bits_of(axis)
    half = value.shape[-1] // 2
    one, two = across_bit(value, axis, first), across_bit(value, axis, second)
    pieces = [(0, 0, value), (first, 0, one), (second, 0, two)]
    last = [
        (first | second, 0, across_bit(one[..., :half], axis, second)),
        (first | second, half, across_bit(two[..., half:], axis, first)),
    ]
    return spread(pieces, axis), last


def spread(pieces, axis):
    for bit in bits_of(axis)[2:]:
        pieces = pieces + [(index | bit, column, across_bit(part, axis, bit)) for index, column, part in pieces]
    return pieces


def chunk_of(index, count):
    return (index & 1) * (count // 2) + (index >> 1)


def bit_scatter(kept, sent, axis, first_fill, second_fill):
    mine = lax.axis_index(axis)
    first, second = bits_of(axis)[:2]
    ways = ((second, first), (first, second))
    comes, first_fill = tie([across_bit(sent[half], axis, now) for half, (now, _) in enumerate(ways)], first_fill)
    stays, comes_last = [], []
    for half, (_, later) in enumerate(ways):
        terms = kept[half] + comes[half].astype(F32)
        is_set = (mine & later) // later
        away = lax.dynamic_index_in_dim(terms, 1 - is_set, 0, keepdims=False).astype(BF16)
        stays.append(lax.dynamic_index_in_dim(terms, is_set, 0, keepdims=False))
        comes_last.append(across_bit(away, axis, later))
    second_fill = second_fill(first_fill)
    comes_last, second_fill = tie(comes_last, second_fill)
    halves = [stay + come.astype(F32) for stay, come in zip(stays, comes_last)]
    return jnp.concatenate(halves, axis=-1), first_fill, second_fill


def shifted(value, axis, steps):
    count = lax.axis_size(axis)
    leading, last = (max(0, -steps), min(count, count - steps))
    return lax.ppermute(value, axis, [(source, source + steps) for source in range(leading, last)])


def to_users(slots, axis):
    count, mine = lax.axis_size(axis), lax.axis_index(axis)
    half = count // 2
    first = lax.ppermute(
        jnp.where(mine < half, slots[0], slots[1]),
        axis,
        [(j, 2 * j if j < half else (2 * j + 1) % count) for j in range(count)],
    )
    second = lax.ppermute(
        jnp.where(mine < half, slots[1], slots[0]),
        axis,
        [(j, 2 * j + 1 if j < half else (2 * j) % count) for j in range(count)],
    )
    even = mine % 2 == 0
    return jnp.where(even, first, second), jnp.where(even, second, first)


def to_owners(block, axis, offset):
    count = lax.axis_size(axis)
    return [
        lax.ppermute(block, axis, [(w, offset + w // 2) for w in range(slot, count, 2)])
        for slot in range(2)
    ]


def tiles_of(width):
    return [pl.ds(at * LANES, LANES) for at in range(width // LANES)]


def row_sums(parts):
    row = lax.broadcasted_iota(jnp.int32, (GROUP, LANES), 0)
    low4, low2, low1 = row < 4, (row & 2) == 0, (row & 1) == 0
    fours = [
        jnp.where(low4, parts[j], parts[j + 4])
        + pltpu.roll(jnp.where(low4, parts[j + 4], parts[j]), 4, 0)
        for j in range(4)
    ]
    twos = [
        jnp.where(low2, fours[j] + pltpu.roll(fours[j], 6, 0), fours[j + 2] + pltpu.roll(fours[j + 2], 2, 0))
        for j in range(2)
    ]
    return jnp.where(low1, twos[0] + pltpu.roll(twos[0], 7, 0), twos[1] + pltpu.roll(twos[1], 1, 0))


def lane_sums(lanes_ref):
    ones = jnp.ones((GROUP, LANES), F32)
    return lax.dot_general(
        ones, lanes_ref[...], (((1,), (1,)), ((), ())), precision=lax.Precision.HIGHEST, preferred_element_type=F32
    )


def summary_kernel(key_ref, keep_ref, rate_ref, feed_ref, decay_ref, state_ref):
    steps, width = rate_ref.shape
    tiles = tiles_of(width)
    keep0, key0 = keep_ref[...], key_ref[...]

    def body(i, carry):
        key, square, keep, decay, state = carry
        decay, state = list(decay), list(state)
        rows = pl.ds(pl.multiple_of(i * GROUP, GROUP), GROUP)
        rate = [rate_ref[rows, tile] for tile in tiles]
        feed = [feed_ref[rows, tile] for tile in tiles]
        for j in range(GROUP):
            key_now, square_now, keep_now = key[:, j : j + 1], square[:, j : j + 1], keep[:, j : j + 1]
            for at in range(len(tiles)):
                factor = keep_now - square_now * rate[at][j : j + 1]
                state[at] = factor * state[at] + key_now * feed[at][j : j + 1]
                decay[at] = factor * decay[at]
        key, square, keep = (pltpu.roll(part, steps - GROUP, 1) for part in (key, square, keep))
        return key, square, keep, tuple(decay), tuple(state)

    zero = jnp.zeros((STATE, LANES), F32)
    start = (key0, keep0 * key0 * key0, keep0, (zero + 1.0,) * len(tiles), (zero,) * len(tiles))
    _, _, _, decay, state = lax.fori_loop(0, steps // GROUP, body, start)
    for at, tile in enumerate(tiles):
        decay_ref[0, :, tile] = decay[at].astype(decay_ref.dtype)
        state_ref[0, :, tile] = state[at].astype(state_ref.dtype)


def adjoint_summary_kernel(key_ref, query_ref, keep_ref, rate_ref, grad_ref, adjoint_ref):
    steps, width = rate_ref.shape
    tiles = tiles_of(width)
    groups = steps // GROUP
    keep0, key0 = keep_ref[...], key_ref[...]

    def body(i, carry):
        square, query, keep, adjoint = carry
        square, query, keep = (pltpu.roll(part, GROUP, 1) for part in (square, query, keep))
        adjoint = list(adjoint)
        rows = pl.ds(pl.multiple_of((groups - 1 - i) * GROUP, GROUP), GROUP)
        rate = [rate_ref[rows, tile] for tile in tiles]
        grad = [grad_ref[rows, tile] for tile in tiles]
        for j in reversed(range(GROUP)):
            square_now, query_now, keep_now = square[:, j : j + 1], query[:, j : j + 1], keep[:, j : j + 1]
            for at in range(len(tiles)):
                full = adjoint[at] + query_now * grad[at][j : j + 1]
                adjoint[at] = (keep_now - square_now * rate[at][j : j + 1]) * full
        return square, query, keep, tuple(adjoint)

    start = (keep0 * key0 * key0, query_ref[...], keep0, (jnp.zeros((STATE, LANES), F32),) * len(tiles))
    adjoint = lax.fori_loop(0, groups, body, start)[-1]
    for at, tile in enumerate(tiles):
        adjoint_ref[0, :, tile] = adjoint[at].astype(adjoint_ref.dtype)


def forward_kernel(key_ref, query_ref, keep_ref, rate_ref, feed_ref, grad_ref, start_ref, out_ref, before_ref, dquery_ref, lanes_ref):
    steps, width = rate_ref.shape
    tiles = tiles_of(width)
    keep0, key0 = keep_ref[...], key_ref[...]

    def body(i, carry):
        key, square, query, keep, state = carry
        state = list(state)
        base = pl.multiple_of(i * GROUP, GROUP)
        rows = pl.ds(base, GROUP)
        rate = [rate_ref[rows, tile] for tile in tiles]
        feed = [feed_ref[rows, tile] for tile in tiles]
        grad = [grad_ref[rows, tile] for tile in tiles]
        weighed = [[] for _ in tiles]
        for j in range(GROUP):
            key_now, square_now = key[:, j : j + 1], square[:, j : j + 1]
            query_now, keep_now = query[:, j : j + 1], keep[:, j : j + 1]
            total = None
            for at, tile in enumerate(tiles):
                before_ref[0, 0, base + j, :, tile] = state[at]
                factor = keep_now - square_now * rate[at][j : j + 1]
                state[at] = factor * state[at] + key_now * feed[at][j : j + 1]
                out = query_now * state[at]
                weighed[at].append(out[:GROUP] + out[GROUP:])
                term = grad[at][j : j + 1] * state[at]
                total = term if total is None else total + term
            lanes_ref[pl.ds(pl.multiple_of((base + j) * STATE, STATE), STATE), :] = total
        for at, tile in enumerate(tiles):
            out_ref[rows, tile] = row_sums(weighed[at])
        key, square, query, keep = (pltpu.roll(part, steps - GROUP, 1) for part in (key, square, query, keep))
        return key, square, query, keep, tuple(state)

    start = tuple(start_ref[0, :, tile] for tile in tiles)
    carry = (key0, keep0 * key0 * key0, query_ref[...], keep0, start)
    lax.fori_loop(0, steps // GROUP, body, carry)
    dquery_ref[...] = lane_sums(lanes_ref)


def backward_kernel(key_ref, query_ref, keep_ref, rate_ref, feed_ref, grad_ref, before_ref, start_ref, along_ref, across_ref, dkey_ref, lanes_ref):
    steps, width = rate_ref.shape
    tiles = tiles_of(width)
    groups = steps // GROUP
    keep0, key0 = keep_ref[...], key_ref[...]

    def body(i, carry):
        key, square, twice, query, keep, adjoint = carry
        key, square, twice, query, keep = (pltpu.roll(part, GROUP, 1) for part in (key, square, twice, query, keep))
        adjoint = list(adjoint)
        base = pl.multiple_of((groups - 1 - i) * GROUP, GROUP)
        rows = pl.ds(base, GROUP)
        rate = [rate_ref[rows, tile] for tile in tiles]
        feed = [feed_ref[rows, tile] for tile in tiles]
        grad = [grad_ref[rows, tile] for tile in tiles]
        along, across = [[None] * GROUP for _ in tiles], [[None] * GROUP for _ in tiles]
        for j in reversed(range(GROUP)):
            key_now, square_now, twice_now = key[:, j : j + 1], square[:, j : j + 1], twice[:, j : j + 1]
            query_now, keep_now = query[:, j : j + 1], keep[:, j : j + 1]
            plain = crossed = None
            for at, tile in enumerate(tiles):
                rate_now = rate[at][j : j + 1]
                full = adjoint[at] + query_now * grad[at][j : j + 1]
                product = full * before_ref[0, 0, base + j, :, tile]
                one, two = key_now * full, square_now * product
                along[at][j] = one[:GROUP] + one[GROUP:]
                across[at][j] = two[:GROUP] + two[GROUP:]
                three, four = full * feed[at][j : j + 1], product * rate_now
                plain = three if plain is None else plain + three
                crossed = four if crossed is None else crossed + four
                adjoint[at] = (keep_now - square_now * rate_now) * full
            lanes_ref[pl.ds(pl.multiple_of((base + j) * STATE, STATE), STATE), :] = plain - twice_now * crossed
        for at, tile in enumerate(tiles):
            along_ref[rows, tile] = row_sums(along[at])
            across_ref[rows, tile] = row_sums(across[at])
        return key, square, twice, query, keep, tuple(adjoint)

    start = tuple(start_ref[0, :, tile] for tile in tiles)
    carry = (
        key0,
        keep0 * key0 * key0,
        2.0 * keep0 * key0,
        query_ref[...],
        keep0,
        start,
    )
    lax.fori_loop(0, groups, body, carry)
    dkey_ref[...] = lane_sums(lanes_ref)


class Mixer:
    def __init__(self, seqs, steps, width):
        self.seqs, self.steps, self.width = seqs, steps, width
        self.part = width
        self.grid = (seqs, width // self.part)
        self.column = pl.BlockSpec((STATE, steps), lambda i, e: (0, i))
        self.row = pl.BlockSpec((steps, self.part), lambda i, e: (i, e))
        self.state = pl.BlockSpec((1, STATE, self.part), lambda i, e: (i, 0, e))
        self.states = pl.BlockSpec((1, 1, steps, STATE, self.part), lambda i, e: (i, e, 0, 0, 0))
        self.sums = pl.BlockSpec((GROUP, steps * STATE), lambda i, e: (e, i))
        self.all_sums = jax.ShapeDtypeStruct((self.grid[1] * GROUP, seqs * steps * STATE), F32)
        self.lanes = pltpu.VMEM((steps * STATE, LANES), F32)
        self.rows = jax.ShapeDtypeStruct((seqs * steps, width), F32)

    def call(self, kernel, name, in_specs, out_specs, out_shape, ops, nbytes, scratch=()):
        elements = self.seqs * self.steps * STATE * self.width
        return pl.pallas_call(
            kernel,
            grid=self.grid,
            in_specs=in_specs,
            out_specs=out_specs,
            out_shape=out_shape,
            name=name,
            scratch_shapes=scratch,
            cost_estimate=pl.CostEstimate(flops=ops * VECTOR_COST * elements, bytes_accessed=nbytes, transcendentals=0),
            compiler_params=pltpu.CompilerParams(
                dimension_semantics=("arbitrary", "arbitrary"), vmem_limit_bytes=48 * 1024 * 1024
            ),
        )

    def summary(self, *args):
        shape = jax.ShapeDtypeStruct((self.seqs, STATE, self.width), BF16)
        specs = [self.column] * 2 + [self.row] * 2
        nbytes = 8 * self.seqs * self.steps * self.width
        return self.call(summary_kernel, "block_summary", specs, [self.state] * 2, [shape] * 2, 6, nbytes)(*args)

    def adjoint_summary(self, *args):
        shape = jax.ShapeDtypeStruct((self.seqs, STATE, self.width), BF16)
        specs = [self.column] * 3 + [self.row] * 2
        nbytes = 8 * self.seqs * self.steps * self.width
        return self.call(adjoint_summary_kernel, "adjoint_summary", specs, self.state, shape, 6, nbytes)(*args)

    def forward(self, *args):
        states = jax.ShapeDtypeStruct((self.seqs, self.grid[1], self.steps, STATE, self.part), F32)
        specs = [self.column] * 3 + [self.row] * 3 + [self.state]
        nbytes = (16 + 4 * STATE) * self.seqs * self.steps * self.width
        return self.call(
            forward_kernel,
            "states",
            specs,
            [self.row, self.states, self.sums],
            [self.rows, states, self.all_sums],
            10,
            nbytes,
            [self.lanes],
        )(*args)

    def columns(self, sums):
        return sum(sums[at * GROUP] for at in range(self.grid[1])).reshape(-1, STATE).T

    def backward(self, *args):
        specs = [self.column] * 3 + [self.row] * 3 + [self.states, self.state]
        nbytes = (20 + 4 * STATE) * self.seqs * self.steps * self.width
        return self.call(
            backward_kernel,
            "adjoints",
            specs,
            [self.row, self.row, self.sums],
            [self.rows, self.rows, self.all_sums],
            20,
            nbytes,
            [self.lanes],
        )(*args)


def copies(pairs, sems):
    moves = [pltpu.make_async_copy(source, target, sems.at[at]) for at, (source, target) in enumerate(pairs)]
    for move in moves:
        move.start()
    return moves


def place_kernel(count, number, where_ref, *refs):
    pieces, gain_ref = refs[:number], refs[number]
    out_ref, raw_ref, normed_ref, sems = refs[-4:]
    gain = gain_ref[...].astype(F32)
    rows = pieces[0].shape[0]
    length = rows - PACKET
    moves = []
    for at, piece_ref in enumerate(pieces):
        for row in range(0, rows, 3 * PACKET):
            piece = piece_ref[row : row + 3 * PACKET, :].astype(F32)
            inverse = lax.rsqrt(jnp.mean(piece * piece, axis=1, keepdims=True) + EPS)
            normed_ref[at, row : row + 3 * PACKET, :] = (piece * inverse * gain).astype(BF16)
        first = pl.multiple_of(where_ref[at] * length, PACKET)
        last = pl.multiple_of(count * length + where_ref[at] * PACKET, PACKET)
        pairs = [
            (normed_ref.at[at, pl.ds(0, length), :], out_ref.at[pl.ds(first, length), :]),
            (normed_ref.at[at, pl.ds(length, PACKET), :], out_ref.at[pl.ds(last, PACKET), :]),
            (piece_ref.at[pl.ds(length, PACKET), :], raw_ref.at[where_ref[at]]),
        ]
        moves += copies(pairs, sems.at[at])
    for move in moves:
        move.wait()


def place(positions, pieces, gain, count, buffers=()):
    rows, model = pieces[0].shape
    number = len(pieces)
    whole = pl.BlockSpec((rows, model), lambda i, where: (0, 0))
    return pl.pallas_call(
        functools.partial(place_kernel, count, number),
        grid_spec=pltpu.PrefetchScalarGridSpec(
            num_scalar_prefetch=1,
            grid=(1,),
            in_specs=[whole] * number
            + [pl.BlockSpec((1, model), lambda i, where: (0, 0))]
            + [pl.BlockSpec(memory_space=pl.ANY)] * len(buffers),
            out_specs=[pl.BlockSpec(memory_space=pl.ANY)] * 2,
            scratch_shapes=[pltpu.VMEM((number, rows, model), BF16), pltpu.SemaphoreType.DMA((number, 3))],
        ),
        out_shape=[
            jax.ShapeDtypeStruct((count * rows, model), BF16),
            jax.ShapeDtypeStruct((count, PACKET, model), BF16),
        ],
        input_output_aliases={2 + number + at: at for at in range(len(buffers))},
        name="place",
        cost_estimate=pl.CostEstimate(flops=rows * model * 8, bytes_accessed=rows * model * 4, transcendentals=rows),
        compiler_params=pltpu.CompilerParams(vmem_limit_bytes=48 * 1024 * 1024),
    )(jnp.stack(positions), *pieces, gain, *buffers)


def project_kernel(plan, where_ref, *refs):
    pieces, normed_ref = refs[: len(plan)], refs[len(plan)]
    out_ref, weight_ref, joined_ref, sems, sem = refs[-5:]
    chunk = pieces[0].shape[1]
    pairs = [
        (
            piece.at[slot],
            joined_ref.at[pl.ds(pl.multiple_of(where_ref[at] * chunk, PACKET), chunk), pl.ds(column, piece.shape[2])],
        )
        for at, (piece, (slot, column)) in enumerate(zip(pieces, plan))
    ]
    for move in copies(pairs, sems):
        move.wait()
    keep = pltpu.make_async_copy(joined_ref, weight_ref, sem)
    keep.start()
    width = joined_ref.shape[0]
    part = min(2 * LANES, width)
    for at in range(0, width, part):
        out_ref[:, at : at + part] = lax.dot_general(
            normed_ref[...], joined_ref[at : at + part, :], (((1,), (1,)), ((), ())), preferred_element_type=F32
        ).astype(out_ref.dtype)
    keep.wait()


def project(slot, positions, pieces, normed, rows, width, dtype):
    model = normed.shape[1]
    plan = [(slot, column) for column, _ in pieces]
    flat = lambda *shape: pl.BlockSpec(shape, lambda i, where: (0, 0))
    return pl.pallas_call(
        functools.partial(project_kernel, plan),
        grid_spec=pltpu.PrefetchScalarGridSpec(
            num_scalar_prefetch=1,
            grid=(1,),
            in_specs=[pl.BlockSpec(memory_space=pl.ANY)] * len(pieces) + [flat(rows, model)],
            out_specs=[flat(rows, width), pl.BlockSpec(memory_space=pl.ANY)],
            scratch_shapes=[
                pltpu.VMEM((width, model), BF16),
                pltpu.SemaphoreType.DMA((len(pieces),)),
                pltpu.SemaphoreType.DMA,
            ],
        ),
        out_shape=[jax.ShapeDtypeStruct((rows, width), dtype), jax.ShapeDtypeStruct((width, model), BF16)],
        name="project",
        cost_estimate=pl.CostEstimate(
            flops=2 * rows * width * model, bytes_accessed=2 * (rows + 2 * width) * model, transcendentals=0
        ),
        compiler_params=pltpu.CompilerParams(vmem_limit_bytes=48 * 1024 * 1024),
    )(jnp.stack(positions), *[piece for _, piece in pieces], normed)


def join_kernel(number, where_ref, *refs):
    pieces, weight_ref = refs[:number], refs[number]
    out_ref, left_ref, joined_ref, sems, sem = refs[-5:]
    rows = pieces[0].shape[0]
    pairs = [
        (piece, joined_ref.at[pl.ds(pl.multiple_of(where_ref[at] * rows, PACKET), rows), :])
        for at, piece in enumerate(pieces)
    ]
    for move in copies(pairs, sems):
        move.wait()
    keep = pltpu.make_async_copy(joined_ref, left_ref, sem)
    keep.start()
    width = weight_ref.shape[0]
    part = min(2 * LANES, width)
    for at in range(0, width, part):
        out_ref[:, at : at + part] = lax.dot_general(
            joined_ref[...], weight_ref[at : at + part, :], (((1,), (1,)), ((), ())), preferred_element_type=F32
        )
    keep.wait()


def join(positions, pieces, weight):
    number = len(pieces)
    rows, model = number * pieces[0].shape[0], pieces[0].shape[1]
    width = weight.shape[0]
    flat = lambda *shape: pl.BlockSpec(shape, lambda i, where: (0, 0))
    return pl.pallas_call(
        functools.partial(join_kernel, number),
        grid_spec=pltpu.PrefetchScalarGridSpec(
            num_scalar_prefetch=1,
            grid=(1,),
            in_specs=[pl.BlockSpec(memory_space=pl.ANY)] * number + [flat(width, model)],
            out_specs=[flat(rows, width), pl.BlockSpec(memory_space=pl.ANY)],
            scratch_shapes=[
                pltpu.VMEM((rows, model), BF16),
                pltpu.SemaphoreType.DMA((number,)),
                pltpu.SemaphoreType.DMA,
            ],
        ),
        out_shape=[jax.ShapeDtypeStruct((rows, width), F32), jax.ShapeDtypeStruct((rows, model), BF16)],
        name="join",
        cost_estimate=pl.CostEstimate(
            flops=2 * rows * width * model, bytes_accessed=2 * (2 * rows + width) * model, transcendentals=0
        ),
        compiler_params=pltpu.CompilerParams(vmem_limit_bytes=48 * 1024 * 1024),
    )(jnp.stack(positions), *pieces, weight)


def widen_kernel(plan, where_ref, *refs):
    pieces, (out_ref, extra_ref, in_ref, wide_ref, in_sems, out_sems, extra_sems) = refs[: len(plan)], refs[-7:]
    rows = out_ref.shape[2]
    steps = [(at, slot) for at in range(len(plan)) for slot in range(pieces[0].shape[0])]

    def load(n):
        at, slot = steps[n]
        size = pieces[at].shape[2]
        return pltpu.make_async_copy(pieces[at].at[slot], in_ref.at[n % DEPTH, :, pl.ds(0, size)], in_sems.at[n % DEPTH])

    def save(n):
        at, slot = steps[n]
        size = pieces[at].shape[2]
        source = wide_ref.at[n % DEPTH]
        target = (slot, where_ref[at], slice(None), pl.ds(plan[at], size))
        return (
            pltpu.make_async_copy(source.at[pl.ds(0, rows), pl.ds(0, size)], out_ref.at[target], out_sems.at[n % DEPTH]),
            pltpu.make_async_copy(
                source.at[pl.ds(rows, extra_ref.shape[2]), pl.ds(0, size)], extra_ref.at[target], extra_sems.at[n % DEPTH]
            ),
        )

    def wait(n):
        for move in save(n):
            move.wait()

    for n in range(min(DEPTH, len(steps))):
        load(n).start()
    for n, (at, _) in enumerate(steps):
        load(n).wait()
        if n >= DEPTH:
            wait(n - DEPTH)
        size = pieces[at].shape[2]
        wide_ref[n % DEPTH, :, :size] = in_ref[n % DEPTH, :, :size].astype(F32)
        for move in save(n):
            move.start()
        if n + DEPTH < len(steps):
            load(n + DEPTH).start()
    for n in range(max(0, len(steps) - DEPTH), len(steps)):
        wait(n)


def widen(pieces, count, rows, buffers=()):
    slots, deep, _ = pieces[0][2].shape
    model = max(column + part.shape[2] for _, column, part in pieces)
    plan = [column for _, column, _ in pieces]
    number = len(pieces)
    return pl.pallas_call(
        functools.partial(widen_kernel, plan),
        grid_spec=pltpu.PrefetchScalarGridSpec(
            num_scalar_prefetch=1,
            grid=(1,),
            in_specs=[pl.BlockSpec(memory_space=pl.ANY)] * (number + len(buffers)),
            out_specs=[pl.BlockSpec(memory_space=pl.ANY)] * 2,
            scratch_shapes=[pltpu.VMEM((DEPTH, deep, model), BF16), pltpu.VMEM((DEPTH, deep, model), F32)]
            + [pltpu.SemaphoreType.DMA((DEPTH,))] * 3,
        ),
        out_shape=[jax.ShapeDtypeStruct((slots, count, size, model), F32) for size in (rows, deep - rows)],
        input_output_aliases={1 + number + at: at for at in range(len(buffers))},
        name="widen",
        cost_estimate=pl.CostEstimate(
            flops=0, bytes_accessed=6 * sum(part.size for _, _, part in pieces), transcendentals=0
        ),
        compiler_params=pltpu.CompilerParams(vmem_limit_bytes=48 * 1024 * 1024),
    )(jnp.stack([position for position, _, _ in pieces]), *[part for _, _, part in pieces], *buffers)


def transposed_dot(left, right):
    return lax.dot_general(left, right, (((0,), (0,)), ((), ())), preferred_element_type=F32)


def shares_kernel(blocks, one_ref, two_ref, one_right_ref, two_right_ref, out_ref):
    chunk = one_ref.shape[1] // blocks

    def put(product):
        for j in range(blocks):
            at = chunk_of(j, blocks) * chunk
            out_ref[0, j * chunk : (j + 1) * chunk, :] = product[at : at + chunk]

    @pl.when(pl.program_id(0) == 0)
    def _():
        put(transposed_dot(one_ref[...], one_right_ref[...]).astype(BF16))

    @pl.when(pl.program_id(0) == 1)
    def _():
        put(transposed_dot(two_ref[...], two_right_ref[...]).astype(BF16))


def shares_of(one, two, one_right, two_right, blocks):
    rows, width = one.shape
    model = one_right.shape[1]
    part = model // 2
    last = model // part - 1
    left = pl.BlockSpec((rows, width), lambda i, j: (0, 0))
    return pl.pallas_call(
        functools.partial(shares_kernel, blocks),
        grid=(2, model // part),
        in_specs=[
            left,
            left,
            pl.BlockSpec((rows, part), lambda i, j: (0, j * (1 - i) + last * i)),
            pl.BlockSpec((rows, part), lambda i, j: (0, j * i)),
        ],
        out_specs=pl.BlockSpec((1, width, part), lambda i, j: (i, 0, j)),
        out_shape=jax.ShapeDtypeStruct((2, width, model), BF16),
        name="shares",
        cost_estimate=pl.CostEstimate(
            flops=4 * rows * width * model, bytes_accessed=4 * (rows + width) * model, transcendentals=0
        ),
        compiler_params=pltpu.CompilerParams(vmem_limit_bytes=48 * 1024 * 1024),
    )(one, two, one_right, two_right)


def terms_kernel(number, groups, where_ref, *refs):
    lefts, rights, (kept_ref, sent_ref, *along, product_ref) = refs[:number], refs[number : 2 * number], refs[2 * number :]
    if along:
        normed_ref, kept_ref, sent_ref, along_ref = kept_ref, sent_ref, *along
    product = jnp.dot(lefts[0][...], rights[0][...], preferred_element_type=F32)
    for left, right in zip(lefts[1:], rights[1:]):
        product = product + jnp.dot(left[...], right[...], preferred_element_type=F32)
    product_ref[...] = product
    if along:
        total = jnp.sum(product * normed_ref[...].astype(F32), axis=0, keepdims=True)
        along_ref[...] = jnp.broadcast_to(total, along_ref.shape)
    length = product_ref.shape[0] // groups
    for r in range(groups):
        part = product_ref[pl.ds(pl.multiple_of(where_ref[r] * length, GROUP), length), :]
        if r % 2:
            sent_ref[r // 2] = part.astype(BF16)
        else:
            kept_ref[r // 2] = part


def terms_of(order, lefts, rights, normed=None):
    groups, number = len(order), len(lefts)
    rows, width = lefts[0].shape
    model = rights[0].shape[1]
    length, part = rows // groups, model // 4
    rounds = pl.BlockSpec((groups // 2, length, part), lambda j, where: (0, 0, j))
    out_specs, out_shape = [rounds, rounds], [
        jax.ShapeDtypeStruct((groups // 2, length, model), dtype) for dtype in (F32, BF16)
    ]
    more = []
    if normed is not None:
        more = [pl.BlockSpec((rows, part), lambda j, where: (0, j))]
        out_specs.append(pl.BlockSpec((GROUP, part), lambda j, where: (0, j)))
        out_shape.append(jax.ShapeDtypeStruct((GROUP, model), F32))
    return pl.pallas_call(
        functools.partial(terms_kernel, number, groups),
        grid_spec=pltpu.PrefetchScalarGridSpec(
            num_scalar_prefetch=1,
            grid=(model // part,),
            in_specs=[pl.BlockSpec((rows, width), lambda j, where: (0, 0))] * number
            + [pl.BlockSpec((width, part), lambda j, where: (0, j))] * number
            + more,
            out_specs=out_specs,
            scratch_shapes=[pltpu.VMEM((rows, part), F32)],
        ),
        out_shape=out_shape,
        name="terms",
        cost_estimate=pl.CostEstimate(
            flops=2 * number * rows * width * model,
            bytes_accessed=number * 2 * (rows + model) * width + 3 * rows * model,
            transcendentals=0,
        ),
        compiler_params=pltpu.CompilerParams(vmem_limit_bytes=48 * 1024 * 1024),
    )(jnp.stack(order), *lefts, *rights, *([] if normed is None else [normed]))


def reorder_kernel(in_ref, out_ref):
    out_ref[...] = in_ref[0].astype(F32)


def reorder(chunks):
    count, rows, model = chunks.shape
    half = count // 2
    return pl.pallas_call(
        reorder_kernel,
        grid=(count,),
        in_specs=[pl.BlockSpec((1, rows, model), lambda j: ((j % half) * 2 + j // half, 0, 0))],
        out_specs=pl.BlockSpec((rows, model), lambda j: (j, 0)),
        out_shape=jax.ShapeDtypeStruct((count * rows, model), F32),
        name="reorder",
        cost_estimate=pl.CostEstimate(flops=0, bytes_accessed=6 * chunks.size, transcendentals=0),
    )(chunks)


def away_kernel(where_ref, left_ref, right_ref, out_ref):
    out_ref[...] = transposed_dot(left_ref[...], right_ref[...]).astype(out_ref.dtype)


def away_product(which, left, right):
    rows, width = left.shape
    model = right.shape[1]
    part, half = model // 2, width // 2
    return pl.pallas_call(
        away_kernel,
        grid_spec=pltpu.PrefetchScalarGridSpec(
            num_scalar_prefetch=1,
            grid=(model // part,),
            in_specs=[
                pl.BlockSpec((rows, half), lambda j, where: (0, where[0])),
                pl.BlockSpec((rows, part), lambda j, where: (0, j)),
            ],
            out_specs=pl.BlockSpec((half, part), lambda j, where: (0, j)),
        ),
        out_shape=jax.ShapeDtypeStruct((half, model), BF16),
        name="away_product",
        cost_estimate=pl.CostEstimate(
            flops=2 * rows * half * model, bytes_accessed=2 * (rows + half) * model, transcendentals=0
        ),
        compiler_params=pltpu.CompilerParams(vmem_limit_bytes=48 * 1024 * 1024),
    )(which.reshape(1), left, right)


def stay_kernel(where_ref, left_ref, right_ref, away_ref, small_ref, small_away_ref, kept_ref, sent_ref):
    product = transposed_dot(left_ref[...], right_ref[...]) + away_ref[...].astype(F32)
    extra = small_ref[...] + small_away_ref[...].astype(F32)
    chunk, more = product.shape[0] // 4, extra.shape[0] // 4
    for at in range(4):
        is_kept = jnp.where(pl.program_id(0) == 0, (at & 1) == where_ref[1], (at >> 1) == where_ref[2])
        index = jnp.where(pl.program_id(0) == 0, at >> 1, at & 1)
        rows = (product[at * chunk : (at + 1) * chunk], extra[at * more : (at + 1) * more])

        @pl.when(is_kept)
        def _():
            kept_ref[0, index, :chunk, :], kept_ref[0, index, chunk:, :] = rows

        @pl.when(jnp.logical_not(is_kept))
        def _():
            sent_ref[0, index, :chunk, :] = rows[0].astype(BF16)
            sent_ref[0, index, chunk:, :] = rows[1].astype(BF16)


def stay_product(which, left, right, away, small, small_away):
    rows, width = left.shape
    model = right.shape[1]
    part, half = model // 2, width // 2
    extra = small.shape[0] // 2
    out = pl.BlockSpec((1, 2, (half + extra) // 4, part), lambda j, where: (j, 0, 0, 0))
    column = lambda size: pl.BlockSpec((size, part), lambda j, where: (0, j))
    return pl.pallas_call(
        stay_kernel,
        grid_spec=pltpu.PrefetchScalarGridSpec(
            num_scalar_prefetch=1,
            grid=(2,),
            in_specs=[
                pl.BlockSpec((rows, half), lambda j, where: (0, where[0])),
                column(rows),
                column(half),
                pl.BlockSpec((extra, part), lambda j, where: (where[0], j)),
                column(extra),
            ],
            out_specs=[out, out],
        ),
        out_shape=[jax.ShapeDtypeStruct((2, 2, (half + extra) // 4, part), dtype) for dtype in (F32, BF16)],
        name="stay_product",
        cost_estimate=pl.CostEstimate(
            flops=2 * rows * half * model, bytes_accessed=2 * (rows + 4 * half) * model, transcendentals=0
        ),
        compiler_params=pltpu.CompilerParams(vmem_limit_bytes=48 * 1024 * 1024),
    )(which, left, right, away, small, small_away)


def terms_kernel(number, groups, where_ref, *refs):
    lefts, rights, (kept_ref, sent_ref, *along, product_ref) = refs[:number], refs[number : 2 * number], refs[2 * number :]
    if along:
        normed_ref, kept_ref, sent_ref, along_ref = kept_ref, sent_ref, *along
    product = jnp.dot(lefts[0][...], rights[0][...], preferred_element_type=F32)
    for left, right in zip(lefts[1:], rights[1:]):
        product = product + jnp.dot(left[...], right[...], preferred_element_type=F32)
    product_ref[...] = product
    if along:
        total = jnp.sum(product * normed_ref[...].astype(F32), axis=0, keepdims=True)
        along_ref[...] = jnp.broadcast_to(total, along_ref.shape)
    length = product_ref.shape[0] // groups
    for r in range(groups):
        part = product_ref[pl.ds(pl.multiple_of(where_ref[r] * length, GROUP), length), :]
        if r % 2:
            sent_ref[r // 2] = part.astype(BF16)
        else:
            kept_ref[r // 2] = part


def terms_of(order, lefts, rights, normed=None):
    groups, number = len(order), len(lefts)
    rows, width = lefts[0].shape
    model = rights[0].shape[1]
    length, part = rows // groups, model // 4
    rounds = pl.BlockSpec((groups // 2, length, part), lambda j, where: (0, 0, j))
    out_specs, out_shape = [rounds, rounds], [
        jax.ShapeDtypeStruct((groups // 2, length, model), dtype) for dtype in (F32, BF16)
    ]
    more = []
    if normed is not None:
        more = [pl.BlockSpec((rows, part), lambda j, where: (0, j))]
        out_specs.append(pl.BlockSpec((GROUP, part), lambda j, where: (0, j)))
        out_shape.append(jax.ShapeDtypeStruct((GROUP, model), F32))
    return pl.pallas_call(
        functools.partial(terms_kernel, number, groups),
        grid_spec=pltpu.PrefetchScalarGridSpec(
            num_scalar_prefetch=1,
            grid=(model // part,),
            in_specs=[pl.BlockSpec((rows, width), lambda j, where: (0, 0))] * number
            + [pl.BlockSpec((width, part), lambda j, where: (0, j))] * number
            + more,
            out_specs=out_specs,
            scratch_shapes=[pltpu.VMEM((rows, part), F32)],
        ),
        out_shape=out_shape,
        name="terms",
        cost_estimate=pl.CostEstimate(
            flops=2 * number * rows * width * model,
            bytes_accessed=number * 2 * (rows + model) * width + 3 * rows * model,
            transcendentals=0,
        ),
        compiler_params=pltpu.CompilerParams(vmem_limit_bytes=48 * 1024 * 1024),
    )(jnp.stack(order), *lefts, *rights, *([] if normed is None else [normed]))


def reorder_kernel(in_ref, out_ref):
    out_ref[...] = in_ref[0].astype(F32)


def reorder(chunks):
    count, rows, model = chunks.shape
    half = count // 2
    return pl.pallas_call(
        reorder_kernel,
        grid=(count,),
        in_specs=[pl.BlockSpec((1, rows, model), lambda j: ((j % half) * 2 + j // half, 0, 0))],
        out_specs=pl.BlockSpec((rows, model), lambda j: (j, 0)),
        out_shape=jax.ShapeDtypeStruct((count * rows, model), F32),
        name="reorder",
        cost_estimate=pl.CostEstimate(flops=0, bytes_accessed=6 * chunks.size, transcendentals=0),
    )(chunks)


def half_kernel(where_ref, left_ref, right_ref, *refs):
    product = transposed_dot(left_ref[...], right_ref[...])
    if len(refs) > 1:
        product = product + refs[0][...].astype(F32)
    refs[-1][...] = product.astype(refs[-1].dtype)


def half_product(which, left, right, dtype, *addend):
    rows, width = left.shape
    model = right.shape[1]
    part, half = model // 2, width // 2
    out = pl.BlockSpec((half, part), lambda j, where: (0, j))
    return pl.pallas_call(
        half_kernel,
        grid_spec=pltpu.PrefetchScalarGridSpec(
            num_scalar_prefetch=1,
            grid=(model // part,),
            in_specs=[
                pl.BlockSpec((rows, half), lambda j, where: (0, where[0])),
                pl.BlockSpec((rows, part), lambda j, where: (0, j)),
            ]
            + [out] * len(addend),
            out_specs=out,
        ),
        out_shape=jax.ShapeDtypeStruct((half, model), dtype),
        name="half_product",
        cost_estimate=pl.CostEstimate(
            flops=2 * rows * half * model, bytes_accessed=2 * (rows + half) * model, transcendentals=0
        ),
        compiler_params=pltpu.CompilerParams(vmem_limit_bytes=48 * 1024 * 1024),
    )(which.reshape(1), left, right, *addend)


def dot(left, right, over_left, over_right):
    return lax.dot_general(left, right, (((over_left,), (over_right,)), ((), ())), preferred_element_type=F32)


def inverse_rms(features):
    return lax.rsqrt(jnp.mean(features * features, axis=1, keepdims=True) + EPS)


def on_device(
    tokens,
    segment_ids,
    norm_gain,
    in_weight,
    conv_weight,
    conv_bias,
    proj_weight,
    dt_weight,
    dt_bias,
    skip_weight,
    out_weight,
    cotangent,
):
    groups, blocks = lax.axis_size("wt"), lax.axis_size("seq")
    mine, block = lax.axis_index("wt"), lax.axis_index("seq")
    own, own_cot, own_ids = tokens[0], cotangent[0], segment_ids[0] + 1
    length, model = own.shape
    width = out_weight.shape[0]
    rows = groups * length
    taps, bias32 = conv_weight.astype(F32), conv_bias.astype(F32)
    dt_bias32, skip32 = dt_bias.astype(F32), skip_weight.astype(F32)

    gain = in_order(small_gather(norm_gain[None], "wt"), "wt").reshape(1, model)
    gain32 = gain.astype(F32)
    chunk = width // blocks
    slots = [lax.dynamic_slice_in_dim(in_weight, slot * width + block * chunk, chunk, 0) for slot in range(2)]
    edge_ids = jnp.pad(own_ids[length - HALO :].astype(BF16), (0, model - HALO))
    packet = jnp.concatenate([own[length - HALO :], edge_ids[None]], axis=0)
    packet, slots = tie(packet, slots)
    packet = shifted(packet, "seq", 1)
    all_ids = jnp.concatenate([packet[HALO, :HALO], own_ids.astype(BF16)])
    ids_row = jnp.pad(all_ids, (0, model - HALO - length))[None]
    sent = jnp.concatenate([own, packet[:HALO], ids_row, jnp.zeros((PACKET - KERNEL, model), BF16)], axis=0)

    value_chunk, gate_chunk = to_users(slots, "wt")
    near_tokens = across_bit(sent, "wt", 1)
    far_tokens = far_gather(sent, "wt")
    value_chunk, near_tokens = tie(value_chunk, near_tokens)
    first_pieces, last_pieces = bit_gather(jnp.stack([value_chunk, gate_chunk]), "seq")
    weight_pieces = first_pieces + spread(last_pieces, "seq")
    chunks = [block ^ r for r, _, _ in weight_pieces]
    parts = [(column, part) for _, column, part in weight_pieces]
    buffers = place([mine, mine ^ 1], [sent, near_tokens], gain, groups)
    far_tokens, buffers = tie(far_tokens, buffers)
    far_tokens.update(near_gather(far_tokens, "wt"))
    order = [mine ^ r for r in range(groups)]
    normed_all, raw_packets = place([mine ^ r for r in far_tokens], list(far_tokens.values()), gain, groups, buffers)
    values_all, value_weight = project(0, chunks, parts, normed_all, normed_all.shape[0], width, BF16)
    extended = jnp.concatenate(
        [
            values_all[rows:].reshape(groups, PACKET, width)[:, :HALO],
            values_all[:rows].reshape(groups, length, width),
        ],
        axis=1,
    ).astype(F32)
    ids = raw_packets[:, HALO, : HALO + length]
    same_doc = [(ids[:, k : k + length] == ids[:, HALO:]).astype(F32)[:, :, None] for k in range(KERNEL)]
    conv_sum = bias32 + sum(taps[k] * extended[:, k : k + length] * same_doc[k] for k in range(KERNEL))
    conv_out = jax.nn.silu(conv_sum).astype(BF16).reshape(rows, width)
    conv_vals = conv_out.astype(F32)

    projected = dot(proj_weight, conv_out, 0, 1)
    projected_sent, late_normed, cot_sent = tie(projected.astype(BF16), normed_all, own_cot)
    projected = all_sum(projected, projected_sent, "wt")
    gate_pre, gate_weight = project(1, chunks, parts, late_normed, rows, width, F32)
    projected, gate_pre = tie(projected, gate_pre)
    cot_pieces = {k: circular(cot_sent, "wt", k) if k else own_cot for k in range(groups)}
    query, key = projected[:STATE], projected[STATE : 2 * STATE]
    low_rank = projected[2 * STATE :].astype(BF16)
    keep = same_doc[KERNEL - 2].reshape(1, rows)
    keeps = jnp.broadcast_to(keep, (STATE, rows))
    key_square = jnp.sum(key * key, axis=0)[:, None]
    beta_in = dot(low_rank, dt_weight, 0, 1) + dt_bias32
    beta = jax.nn.softplus(beta_in)
    shrink = 1.0 / (1.0 + beta * key_square)
    rate = beta * shrink
    feed = rate * conv_vals
    mixer = Mixer(groups, length, width)
    own_map = jnp.stack(mixer.summary(key, keeps, rate, feed))
    cot_pieces, own_map = tie(cot_pieces, own_map)
    maps = lax.all_gather(own_map, "seq")
    d_gated, cots = join([(mine - k) % groups for k in cot_pieces], list(cot_pieces.values()), out_weight)
    sigma = jax.nn.sigmoid(gate_pre)
    gate = gate_pre * sigma
    d_mixed = d_gated * gate
    adjoint = mixer.adjoint_summary(key, query, keeps, rate, d_mixed)
    adjoints = lax.all_gather(adjoint, "seq")
    state_in = jnp.zeros((groups, STATE, width), F32)
    for at in range(blocks):
        step = maps[at, 0].astype(F32) * state_in + maps[at, 1].astype(F32)
        state_in = jnp.where(at < block, step, state_in)

    core_out, before, d_query = mixer.forward(key, query, keeps, rate, feed, d_mixed, state_in)
    adjoints, core_out = tie(adjoints, core_out)
    grad_in = jnp.zeros((groups, STATE, width), F32)
    for at in reversed(range(blocks)):
        step = maps[at, 0].astype(F32) * grad_in + adjoints[at].astype(F32)
        grad_in = jnp.where(at > block, step, grad_in)
    d_query = mixer.columns(d_query)
    mixed = core_out + skip32 * conv_vals
    gated = (mixed * gate).astype(BF16)
    d_gate = (d_gated * mixed * (sigma * (1.0 + gate_pre * (1.0 - sigma)))).astype(BF16)
    skip_part = jnp.sum(d_mixed * conv_vals, axis=0)
    shares = shares_of(gated, d_gate, cots, normed_all, blocks)
    out_kept, out_sent = terms_of(order, [gated], [out_weight])
    shares, out_sent, grad_in = tie(shares, out_sent, grad_in)
    out_chunk, gate_part = lax.psum_scatter(shares, "seq", scatter_dimension=1, tiled=True)
    out_comes = across_bit(out_sent, "wt", 1)
    gate_slots = to_owners(gate_part, "wt", groups // 2)

    along, across, d_key = mixer.backward(key, query, keeps, rate, feed, d_mixed, before, grad_in)
    along, across, d_key, out_comes = tie(along, across, d_key, out_comes)
    d_key = mixer.columns(d_key)
    d_rate = conv_vals * along - across
    d_beta = d_rate * shrink * shrink
    from_square = jnp.sum(d_beta * beta * beta, axis=1)
    d_key = d_key - 2.0 * key * from_square
    d_bias = d_beta * jax.nn.sigmoid(beta_in)
    dt_bias_part = jnp.sum(d_bias, axis=0)
    d_beta_low = d_bias.astype(BF16)
    d_low_rank = dot(dt_weight, d_beta_low, 0, 1)
    d_projected = jnp.concatenate([d_query, d_key, d_low_rank], axis=0)
    out_terms = near_sum(out_kept, out_comes)
    d_projected = all_sum(d_projected, d_projected.astype(BF16), "wt").astype(BF16)
    d_projected, out_sent = tie(d_projected, out_terms[-1].astype(BF16))
    dt_part = dot(low_rank, d_beta_low, 1, 0)
    proj_part = dot(d_projected, conv_out, 1, 0)
    d_value = d_mixed * skip32 + rate * along + dot(d_projected, proj_weight, 0, 1)

    sigma_conv = jax.nn.sigmoid(conv_sum)
    d_conv = d_value.reshape(groups, length, width) * (sigma_conv * (1.0 + conv_sum * (1.0 - sigma_conv)))
    conv_bias_part = jnp.sum(d_conv, axis=(0, 1))
    masked = [d_conv * same_doc[k] for k in range(KERNEL)]
    conv_part = jnp.stack([jnp.sum(masked[k] * extended[:, k : k + length], axis=(0, 1)) for k in range(KERNEL)])
    d_extended = sum(
        jnp.pad(taps[k] * masked[k], ((0, 0), (k, HALO - k), (0, 0))) for k in range(KERNEL)
    )
    returned = shifted(d_extended[:, :HALO], "seq", -1)
    d_rows = d_extended[:, HALO:] + jnp.pad(returned, ((0, 0), (length - HALO, 0), (0, 0)))
    d_rows = d_rows.astype(BF16).reshape(rows, width)

    upper, lower, lowest = (block & (blocks // 2)) // (blocks // 2), (block & (blocks // 4)) // (blocks // 4), block & 1
    away = across_bit(away_product(1 - lowest, d_rows, normed_all), "seq", 1)
    one_rows = jnp.concatenate([conv_part, jnp.stack([conv_bias_part, dt_bias_part, skip_part, jnp.zeros_like(skip_part)])])
    deep, folds = PACKET * 2 * blocks, model // width
    flat = jnp.concatenate([proj_part, dt_part, one_rows], axis=0)
    flat = jnp.pad(flat, ((0, folds * deep - flat.shape[0]), (0, 0)))
    small = jnp.concatenate([flat[at * deep : (at + 1) * deep] for at in range(folds)], axis=1)
    small_sent = lax.dynamic_slice_in_dim(small, (1 - lowest) * (deep // 2), deep // 2, 0).astype(BF16)
    small_away = across_bit(small_sent, "seq", 1)
    which = jnp.stack([lowest, lower, upper])
    kept, sent = stay_product(which, d_rows, normed_all, away, small, small_away)
    late_rows, kept = tie(d_rows, kept)
    d_normed_terms = terms_of(order, [late_rows, d_gate], [value_weight, gate_weight], normed_all)

    def then_output(_):
        return (own.astype(F32) + far_sum(out_terms, "wt", out_sent)).astype(BF16)

    summed, d_normed_terms, block_output = bit_scatter(kept, sent, "seq", d_normed_terms, then_output)
    d_normed_kept, d_normed_sent, gain_part = d_normed_terms
    own_rows = (width // 8, deep // 8)
    for bit in bits_of("seq")[2:-1]:
        is_set = (block & bit) // bit
        terms = [summed[: own_rows[0]], summed[own_rows[0] :]]
        own_rows = (own_rows[0] // 2, own_rows[1] // 2)
        pick = lambda want: jnp.concatenate(
            [lax.dynamic_slice_in_dim(part, want * size, size, 0) for part, size in zip(terms, own_rows)]
        )
        summed = pick(is_set) + across_bit(pick(1 - is_set).astype(BF16), "seq", bit).astype(F32)
    summed = summed.astype(BF16)
    value_slots = to_owners(summed[:chunk], "wt", 0)
    small_slots = summed[chunk:].reshape(2, PACKET, model)

    d_normed_comes = across_bit(d_normed_sent, "wt", 1)

    value_slots, d_normed_comes = tie(value_slots, d_normed_comes)
    in_chunk = jnp.stack([jnp.concatenate([value_slots[slot] + gate_slots[slot], small_slots[slot]]) for slot in range(2)])
    placed = lambda pieces: [(chunk_of(block ^ r, blocks), column, part) for r, column, part in pieces]
    first_pieces, last_pieces = bit_gather(in_chunk, "seq")
    buffers = widen(placed(first_pieces), blocks, chunk)

    held = []

    def hold(part):
        part, *rest = tie(part, *(held or buffers))
        held[:] = rest
        return part

    d_normed = far_sum(near_sum(d_normed_kept, d_normed_comes), "wt", hold=hold)
    buffers = held
    own32 = own.astype(F32)
    inv_rms = inverse_rms(own32)
    weighted = d_normed * gain32
    along_features = jnp.mean(own32 * weighted, axis=1, keepdims=True)
    token_grad = (own_cot.astype(F32) + inv_rms * weighted - own32 * (inv_rms * inv_rms * inv_rms) * along_features).astype(BF16)
    gain_part = gain_part[0] / gain32[0]
    gain_stays, gain_comes = direct_scatter(gain_part.reshape(groups, 1, model // groups), "wt")
    gain_grad = (gain_stays + sum(part.astype(F32) for part in gain_comes))[0]
    for bit in bits_of("seq"):
        gain_grad = gain_grad + across_bit(gain_grad, "seq", bit)
    out_grad = reorder(lax.all_gather(out_chunk, "seq"))
    last_parts, *buffers, out_grad = tie([part for _, _, part in last_pieces], *buffers, out_grad)
    last_pieces = [(r, column, part) for (r, column, _), part in zip(last_pieces, last_parts)]
    in_grad, small = widen(placed(spread(last_pieces, "seq")), blocks, chunk, buffers)
    in_grad = in_grad.reshape(2 * width, model)
    small = small.transpose(1, 0, 2, 3).reshape(deep, model)
    flat = jnp.concatenate([small[:, at * width : (at + 1) * width] for at in range(folds)], axis=0)
    ranks, low_ranks = proj_part.shape[0], dt_part.shape[0]
    proj_grad, dt_grad, small = flat[:ranks].T, flat[ranks : ranks + low_ranks].T, flat[ranks + low_ranks :]
    conv_grad, conv_bias_grad, dt_bias_grad, skip_grad = small[:KERNEL], small[KERNEL], small[KERNEL + 1], small[KERNEL + 2]
    return (
        block_output[None],
        token_grad[None],
        gain_grad,
        in_grad,
        conv_grad,
        conv_bias_grad,
        proj_grad,
        dt_grad,
        dt_bias_grad,
        skip_grad,
        out_grad,
    )


def solution(mesh):
    return jax.shard_map(
        on_device,
        mesh=mesh,
        in_specs=(
            P("wt", "seq", None),
            P("wt", "seq"),
            P("wt"),
            P("wt", None),
            P(None, "wt"),
            P("wt"),
            P("wt", None),
            P("wt", None),
            P("wt"),
            P("wt"),
            P("wt", None),
            P("wt", "seq", None),
        ),
        out_specs=(
            P("wt", "seq", None),
            P("wt", "seq", None),
            P("wt"),
            P("wt", None),
            P(None, "wt"),
            P("wt"),
            P("wt", None),
            P("wt", None),
            P("wt"),
            P("wt"),
            P("wt", None),
        ),
        check_vma=False,
    )
```
